32 devices in a mesh: row: 4 (over z), col: 8 (over y, x, core).
Axes of the slice: x: 2, y: 2, z: 4, core: 2. Of those that a mesh axis runs over, the one named last changes fastest.
Arguments:
- matrix: float32 [4, 1024, 2, 2048], P(None, 'row', None, 'col'), may hold values from -6 to 6, as said below
Outputs:
- factored: float32 [4, 1024, 2, 2048], P(None, 'row', None, 'col')
The draws below stay inside these ranges and needn't reach their ends.
Inputs may be any that keep to these rules, and one draw needn't show every extreme that they name: symmetric; the leading 2 * 256 rows and columns form a positive definite matrix.
All inputs are finite; a program needn't handle non-finite values.
Results may differ from the reference program's by a relative error of at most 0.0001.
Values sent between devices are 32-bit elements; how exact they have to be, the bound alone decides.
A program may use at most 64 MiB of HBM per device.

```python
import jax
import jax.numpy as jnp
from jax import lax

B = 256
BC = 2
PANELS = 2
BR = 4
ORDER = 4096
N_ROW = 4
N_COL = 8


def draw_matrix(key, part):
    first_key, second_key = jax.random.split(key)
    leading = PANELS * B
    base = jnp.clip(jax.random.normal(first_key, (ORDER, ORDER), jnp.float32), -6.0, 6.0)
    sym = (base + base.T) * 0.5
    index = jnp.arange(ORDER)
    inner = index < leading
    both_in = inner[:, None] & inner[None, :]
    both_out = (~inner)[:, None] & (~inner)[None, :]
    diag_values = 2.0 + 2.0 * jax.random.uniform(second_key, (ORDER,), jnp.float32)
    lead_part = 1.9 / leading * jnp.tanh(sym)
    trailing = sym
    result = jnp.where(both_in, lead_part, jnp.where(both_out, trailing, 0.25 * sym))
    on_diag = (index[:, None] == index[None, :]) & both_in
    result = jnp.where(on_diag, diag_values[None, :], result)
    return result.astype(jnp.float32).reshape(BR, N_ROW * B, BC, N_COL * B)


def setup_inputs(seed: int = 0) -> dict:
    seeds = jax.random.split(jax.random.key(seed), 2)
    return {
        "matrix": draw_matrix(jax.random.fold_in(seeds[1], 71), 0),
    }


def reference(matrix):
    full = matrix.reshape(ORDER, ORDER)
    for panel in range(PANELS):
        start = panel * B
        stop = start + B
        diag_factor = jnp.linalg.cholesky(full[start:stop, start:stop])
        below = lax.linalg.triangular_solve(diag_factor, full[stop:, start:stop], left_side=False, lower=True, transpose_a=True)
        trailing = full[stop:, stop:] - jnp.dot(below.astype(jnp.float32), below.T.astype(jnp.float32), precision=lax.Precision.HIGHEST, preferred_element_type=jnp.float32)
        column = jnp.concatenate((jnp.zeros((start, B), jnp.float32), diag_factor, below), axis=0)
        full = full.at[:, start:stop].set(column)
        full = full.at[start:stop, stop:].set(jnp.zeros((B, ORDER - stop), jnp.float32))
        full = full.at[stop:, stop:].set(trailing)
    return full.reshape(BR, N_ROW * B, BC, N_COL * B)
```

```python
import functools
import math

import jax
import jax.numpy as jnp
from jax import lax
from jax.experimental import pallas as pl
from jax.experimental.pallas import tpu as pltpu
from jax.sharding import PartitionSpec as P

MESH = pl.DeviceIdType.MESH
PANELS = 2
PIECES = 2
GROUP = 8
HIGHEST = lax.Precision.HIGHEST


def mm(a, b):
    return jnp.dot(a, b, precision=HIGHEST, preferred_element_type=jnp.float32)


def mm_nt(a, b):
    return lax.dot_general(
        a, b, (((1,), (1,)), ((), ())), precision=HIGHEST, preferred_element_type=jnp.float32
    )


def mm_tn(a, b):
    return lax.dot_general(
        a, b, (((0,), (0,)), ((), ())), precision=HIGHEST, preferred_element_type=jnp.float32
    )


def snake(pos, width):
    major, minor = pos // width, pos % width
    return major, jnp.where(major % 2 == 0, minor, width - 1 - minor)


def exchange(shape, m_ref, cols, rows, lead, x_send, x_recv, p_send, p_recv, l_up, l_down, l_recv,
             lp_send, lp_recv, r_up, r_down, r_recv):
    n_row, n_col = shape
    chips = n_col // 2
    width = math.isqrt(chips)
    if width * width != chips:
        width = chips
    height = chips // width
    z = lax.axis_index("row")
    col = lax.axis_index("col")
    chip, core = col // 2, col % 2
    partner = (z, chip * 2 + 1 - core)
    y, x = chip // width, chip % width
    pos_a = y * width + jnp.where(y % 2 == 0, x, width - 1 - x)
    pos_b = x * height + jnp.where(x % 2 == 0, y, height - 1 - y)
    pos = jnp.where(core == 0, pos_a, pos_b)

    def chip_at(p):
        ya, xa = snake(p, width)
        xb, yb = snake(p, height)
        return jnp.where(core == 0, ya * width + xa, yb * width + xb)

    last = chips - 1
    has_next, has_prev = pos < last, pos > 0
    nxt = (z, chip_at(jnp.minimum(pos + 1, last)) * 2 + core)
    prv = (z, chip_at(jnp.maximum(pos - 1, 0)) * 2 + core)
    up, down = (z + 1, col), (z - 1, col)
    has_up, has_down = z < n_row - 1, z > 0

    barrier = pltpu.get_barrier_semaphore()

    def greet(cond, dev):
        @pl.when(cond)
        def _():
            pl.semaphore_signal(barrier, inc=1, device_id=dev, device_id_type=MESH)

    pl.semaphore_signal(barrier, inc=1, device_id=partner, device_id_type=MESH)
    greet(has_next, nxt)
    greet(has_prev, prv)
    greet(has_up, up)
    greet(has_down, down)
    one = lambda c: jnp.where(c, 1, 0)
    pl.semaphore_wait(barrier, 1 + one(has_next) + one(has_prev) + one(has_up) + one(has_down))

    def rcopy(src, dst, s, r, dev):
        return pltpu.make_async_remote_copy(
            src_ref=src, dst_ref=dst, send_sem=s, recv_sem=r, device_id=dev, device_id_type=MESH
        )

    blocks, size = m_ref.shape[0], m_ref.shape[2]
    step = size // PIECES

    def part(t):
        return t // PIECES, pl.ds((t % PIECES) * step, step)

    def x_copies(t, own):
        a, d = part(t)
        src = m_ref.at[a, 0, d] if own else cols.at[core, a, d]
        dst = cols.at[core, a, d]
        return (rcopy(src, dst, x_send.at[t], x_recv.at[t], nxt),
                rcopy(src, dst, p_send.at[t], p_recv.at[t], partner))

    def x_piece(t):
        @pl.when(jnp.logical_not(has_prev))
        def _():
            chain, side = x_copies(t, True)
            chain.start()
            side.start()

        @pl.when(has_prev)
        def _():
            chain, side = x_copies(t, False)
            chain.wait_recv()

            @pl.when(has_next)
            def _():
                chain.start()
            side.start()

    def r_copy(k, u, own, is_up):
        c, d = part(u)
        src = m_ref.at[0, c, d] if own else rows.at[k, c, d]
        sem = r_up.at[k, u] if is_up else r_down.at[u]
        return rcopy(src, rows.at[k, c, d], sem, r_recv.at[k, u], up if is_up else down)

    n_r = m_ref.shape[1] * PIECES

    def r_start(u):
        @pl.when(z == 0)
        def _():
            r_copy(0, u, True, True).start()

        @pl.when(z == 1)
        def _():
            r_copy(1, u, True, False).start()

            @pl.when(has_up)
            def _():
                r_copy(1, u, True, True).start()

    def r_relay(k, u):
        @pl.when(z != k)
        def _():
            r_copy(k, u, False, True).wait_recv()

        @pl.when((z > k) & has_up)
        def _():
            r_copy(k, u, False, True).start()

    origin = (0, 1, 1)
    carrier = (0, 0, 1)

    def l_copy(b, own, is_up):
        src = cols.at[carrier[b], 0] if own == 2 else (m_ref.at[0, 0] if own == 1 else lead.at[b])
        sem = l_up.at[b] if is_up else l_down.at[b]
        return rcopy(src, lead.at[b], sem, l_recv.at[b], up if is_up else down)

    def l_side(b):
        return rcopy(lead.at[b], lead.at[b], lp_send.at[b], lp_recv.at[b], partner)

    def l_start(b):
        for own, cond in ((2, has_prev), (1, jnp.logical_not(has_prev))):
            @pl.when((z == origin[b]) & (core == carrier[b]) & cond)
            def _():
                if origin[b] > 0:
                    l_copy(b, own, False).start()

                @pl.when(has_up)
                def _():
                    l_copy(b, own, True).start()

    def l_relay(b):
        @pl.when((z != origin[b]) & (core == carrier[b]))
        def _():
            l_copy(b, 0, True).wait_recv()

            @pl.when((z > origin[b]) & has_up)
            def _():
                l_copy(b, 0, True).start()
            l_side(b).start()

        @pl.when((z != origin[b]) & (core != carrier[b]))
        def _():
            l_side(b).wait_recv()

    n_x = blocks * PIECES
    for t in range(PIECES):
        x_piece(t)
    for b in range(3):
        l_start(b)
    for u in range(n_r):
        r_start(u)
    for t in range(PIECES, 2 * PIECES):
        x_piece(t)
    for b in range(3):
        l_relay(b)
    plan = [functools.partial(r_relay, k, u) for u in range(n_r) for k in range(2)]
    for t in range(2 * PIECES, n_x):
        x_piece(t)
        if plan:
            plan.pop(0)()
        if plan:
            plan.pop(0)()
    for job in plan:
        job()

    for t in range(n_x):
        a, d = part(t)
        other = cols.at[1 - core, a, d]
        rcopy(other, other, p_send.at[t], p_recv.at[t], partner).wait_recv()
    for t in range(n_x):
        chain, side = x_copies(t, False)
        side.wait_send()

        @pl.when(has_next)
        def _():
            chain.wait_send()
    for u in range(n_r):
        @pl.when(has_up)
        def _():
            r_copy(0, u, False, True).wait_send()

        @pl.when(has_up & (z > 0))
        def _():
            r_copy(1, u, False, True).wait_send()

        @pl.when(z == 1)
        def _():
            r_copy(1, u, False, False).wait_send()
    for b in range(3):
        @pl.when((core == carrier[b]) & (z >= origin[b]) & has_up)
        def _():
            l_copy(b, 0, True).wait_send()

        @pl.when((core == carrier[b]) & (z != origin[b]))
        def _():
            l_side(b).wait_send()
        if origin[b] > 0:
            @pl.when((core == carrier[b]) & (z == origin[b]))
            def _():
                l_copy(b, 0, False).wait_send()

    @pl.when(jnp.logical_not(has_prev))
    def _():
        for a in range(blocks):
            cols[core, a] = m_ref[a, 0]

    for k in range(2):
        @pl.when(z == k)
        def _():
            rows[k] = m_ref[0]
    for b in range(3):
        @pl.when(z == origin[b])
        def _():
            lead[b] = cols[carrier[b], 0]


def factor_small(s_ref):
    n = s_ref.shape[0]
    lane = lax.broadcasted_iota(jnp.int32, (GROUP, n), 1)

    def step(i, carry):
        base = pl.multiple_of(i * GROUP, GROUP)
        g = s_ref[pl.ds(base, GROUP), :]
        diag = pltpu.roll(g[:, :n], lax.rem(n - base, n), 1)
        t = {}
        for a in range(GROUP):
            for b in range(a + 1):
                t[a, b] = jnp.broadcast_to(diag[b:b + 1, a:a + 1], (1, n))
        left = [g[a:a + 1, :n] for a in range(GROUP)]
        right = [g[a:a + 1, n:] for a in range(GROUP)]
        for k in range(GROUP):
            r = lax.rsqrt(t[k, k])
            left[k] = left[k] * r
            right[k] = right[k] * r
            col = {a: t[a, k] * r for a in range(k + 1, GROUP)}
            for a in range(k + 1, GROUP):
                for b in range(k + 1, a + 1):
                    t[a, b] = t[a, b] - col[a] * col[b]
            for a in range(k + 1, GROUP):
                left[a] = left[a] - col[a] * left[k]
                right[a] = right[a] - col[a] * right[k]
        u = jnp.concatenate(left, axis=0)
        v = jnp.concatenate(right, axis=0)
        done = jnp.concatenate([u, v], axis=1)
        s_ref[pl.ds(base, GROUP), :] = done

        def split(w):
            h = w.astype(jnp.bfloat16).astype(jnp.float32)
            rest = w - h
            m = rest.astype(jnp.bfloat16).astype(jnp.float32)
            return h, m, rest - m

        h, m, l = split(done)
        keep = lane >= base + GROUP
        hm, mm_, lm = (jnp.where(keep, w[:, :n], 0.0) for w in (h, m, l))
        lhs = jnp.concatenate([hm, hm, mm_, hm, lm, mm_], axis=0).astype(jnp.bfloat16)
        rhs = jnp.concatenate([h, m, h, l, h, m], axis=0).astype(jnp.bfloat16)
        s_ref[...] -= lax.dot_general(
            lhs, rhs, (((0,), (0,)), ((), ())), preferred_element_type=jnp.float32
        )
        return carry

    lax.fori_loop(0, n // GROUP, step, 0)


def factor(src, low, inv, s_ref):
    size = src.shape[0]
    n = s_ref.shape[0]
    row = lax.broadcasted_iota(jnp.int32, (n, n), 0)
    lane = lax.broadcasted_iota(jnp.int32, (n, n), 1)
    eye = jnp.where(row == lane, 1.0, 0.0)
    low[...] = jnp.zeros_like(low)
    inv[...] = jnp.zeros_like(inv)
    for b in range(size // n):
        at = slice(b * n, (b + 1) * n)
        s_ref[:, :n] = src[at, at]
        s_ref[:, n:] = eye
        factor_small(s_ref)
        v = jnp.where(row >= lane, s_ref[:, n:], 0.0)
        low[at, at] = jnp.where(row <= lane, s_ref[:, :n], 0.0).T
        inv[at, at] = v
        if b > 0:
            inv[at, :b * n] = -mm(v, mm(low[at, :b * n], inv[:b * n, :b * n]))
        if (b + 1) * n < size:
            below = mm_nt(src[(b + 1) * n:, at], v)
            low[(b + 1) * n:, at] = below
            src[(b + 1) * n:, (b + 1) * n:] -= mm_nt(below, below)


def compute(shape, m_ref, cols, rows, lead, out, work, low, inv, l10, q, s_ref):
    n_row, n_col = shape
    z = lax.axis_index("row")
    col = lax.axis_index("col")
    blocks, per = m_ref.shape[0], m_ref.shape[1]
    work[...] = lead[0]
    factor(work, low.at[0], inv.at[0], s_ref)
    l10[...] = mm_nt(lead[1], inv[0])
    work[...] = lead[2] - mm_nt(l10[...], l10[...])
    factor(work, low.at[1], inv.at[1], s_ref)
    for c in range(per):
        q[0, c] = mm(inv[0], rows[0, c])
        q[1, c] = mm(inv[1], rows[1, c] - mm(l10[...], q[0, c]))

    def block_row(a, carry):
        p0 = mm_nt(cols[0, a], inv[0])
        p1 = mm_nt(cols[1, a] - mm_nt(p0, l10[...]), inv[1])
        for c in range(per):
            out[a, c] = m_ref[a, c] - mm(p0, q[0, c]) - mm(p1, q[1, c])

        @pl.when(col == 0)
        def _():
            out[a, 0] = p0

        @pl.when(col == 1)
        def _():
            out[a, 0] = p1
        return carry

    lax.fori_loop(0, blocks, block_row, 0)

    @pl.when(z < PANELS)
    def _():
        out[0] = jnp.zeros_like(out[0])

        @pl.when((z == 0) & (col == 0))
        def _():
            out[0, 0] = low[0]

        @pl.when((z == 1) & (col == 0))
        def _():
            out[0, 0] = l10[...]

        @pl.when((z == 1) & (col == 1))
        def _():
            out[0, 0] = low[1]


def shards(shape, matrix):
    m = matrix.transpose(0, 2, 1, 3)
    blocks, per, size, _ = m.shape
    f32 = jnp.float32
    dma = pltpu.SemaphoreType.DMA
    n_x, n_r = blocks * PIECES, per * PIECES
    vmem = pl.BlockSpec(memory_space=pltpu.VMEM)
    cols, rows, lead = pl.pallas_call(
        functools.partial(exchange, shape),
        out_shape=(jax.ShapeDtypeStruct((2, blocks, size, size), f32),
                   jax.ShapeDtypeStruct((2, per, size, size), f32),
                   jax.ShapeDtypeStruct((3, size, size), f32)),
        in_specs=[vmem],
        out_specs=(vmem, vmem, vmem),
        scratch_shapes=[dma((n_x,))] * 4 + [dma((3,))] * 5 + [dma((2, n_r)), dma((n_r,)), dma((2, n_r))],
        compiler_params=pltpu.CompilerParams(collective_id=0, has_side_effects=True),
        name="exchange",
    )(m)
    tile = 128
    out = pl.pallas_call(
        functools.partial(compute, shape),
        out_shape=jax.ShapeDtypeStruct(m.shape, f32),
        in_specs=[vmem] * 4,
        out_specs=vmem,
        scratch_shapes=[
            pltpu.VMEM((size, size), f32),
            pltpu.VMEM((2, size, size), f32),
            pltpu.VMEM((2, size, size), f32),
            pltpu.VMEM((size, size), f32),
            pltpu.VMEM((2, per, size, size), f32),
            pltpu.VMEM((tile, 2 * tile), f32),
        ],
        name="compute",
    )(m, cols, rows, lead)
    return out.transpose(0, 2, 1, 3)


def solution(mesh):
    spec = P(None, "row", None, "col")
    shape = (mesh.shape["row"], mesh.shape["col"])
    return jax.shard_map(
        functools.partial(shards, shape), mesh=mesh, in_specs=(spec,), out_specs=spec, check_vma=False
    )
```

```python
import functools
import math

import jax
import jax.numpy as jnp
from jax import lax
from jax.experimental import pallas as pl
from jax.experimental.pallas import tpu as pltpu
from jax.sharding import PartitionSpec as P

MESH = pl.DeviceIdType.MESH
PANELS = 2
PIECES = 4
R_PIECES = 2
STEPS = 4
GROUP = 8
HIGHEST = lax.Precision.HIGHEST


def mm(a, b):
    return jnp.dot(a, b, precision=HIGHEST, preferred_element_type=jnp.float32)


def mm_nt(a, b):
    return lax.dot_general(
        a, b, (((1,), (1,)), ((), ())), precision=HIGHEST, preferred_element_type=jnp.float32
    )


def mm_tn(a, b):
    return lax.dot_general(
        a, b, (((0,), (0,)), ((), ())), precision=HIGHEST, preferred_element_type=jnp.float32
    )


def snake(pos, width):
    major, minor = pos // width, pos % width
    return major, jnp.where(major % 2 == 0, minor, width - 1 - minor)


class Exchange:
    def __init__(self, shape, m_ref, cols, rows, lead, sems):
        (self.x_send, self.x_recv, self.p_send, self.p_recv, self.l_up, self.l_down, self.l_side,
         self.l_recv, self.lp_send, self.lp_recv, self.r_up, self.r_down, self.r_recv) = sems
        self.m, self.cols, self.rows, self.lead = m_ref, cols, rows, lead
        n_row, n_col = shape
        self.n_row, self.n_col = shape
        chips = n_col // 2
        width = math.isqrt(chips)
        if width * width != chips:
            width = chips
        height = chips // width
        z = lax.axis_index("row")
        col = lax.axis_index("col")
        chip, core = col // 2, col % 2
        y, x = chip // width, chip % width
        pos_a = y * width + jnp.where(y % 2 == 0, x, width - 1 - x)
        pos_b = x * height + jnp.where(x % 2 == 0, y, height - 1 - y)
        pos = jnp.where(core == 0, pos_a, pos_b)

        def chip_at(p):
            ya, xa = snake(p, width)
            xb, yb = snake(p, height)
            return jnp.where(core == 0, ya * width + xa, yb * width + xb)

        last = chips - 1
        self.z, self.col, self.core = z, col, core
        self.odd = chip % 2 == 1
        self.partner = (z, chip * 2 + 1 - core)
        self.beside = (z, (chip + 1 - 2 * (chip % 2)) * 2 + core)
        self.has_next, self.has_prev = pos < last, pos > 0
        self.nxt = (z, chip_at(jnp.minimum(pos + 1, last)) * 2 + core)
        prv = (z, chip_at(jnp.maximum(pos - 1, 0)) * 2 + core)
        self.up, self.down = (z + 1, col), (z - 1, col)
        self.has_up, has_down = z < n_row - 1, z > 0
        self.blocks, self.per, self.size = m_ref.shape[0], m_ref.shape[1], m_ref.shape[2]
        self.n_x = self.blocks * PIECES
        self.n_r = self.per * R_PIECES
        self.home = col % n_row
        self.late = self.home >= PANELS

        barrier = pltpu.get_barrier_semaphore()

        def greet(cond, dev):
            @pl.when(cond)
            def _():
                pl.semaphore_signal(barrier, inc=1, device_id=dev, device_id_type=MESH)

        for dev in (self.partner, self.beside):
            pl.semaphore_signal(barrier, inc=1, device_id=dev, device_id_type=MESH)
        near = ((self.has_next, self.nxt), (self.has_prev, prv), (self.has_up, self.up),
                (has_down, self.down))
        count = 2
        for cond, dev in near:
            greet(cond, dev)
            count = count + jnp.where(cond, 1, 0)
        pl.semaphore_wait(barrier, count)

    def copy(self, src, dst, s, r, dev):
        return pltpu.make_async_remote_copy(
            src_ref=src, dst_ref=dst, send_sem=s, recv_sem=r, device_id=dev, device_id_type=MESH
        )

    def part(self, t, pieces):
        step = self.size // pieces
        return t // pieces, pl.ds((t % pieces) * step, step)

    def x_copies(self, t, own):
        a, d = self.part(t, PIECES)
        dst = self.cols.at[self.core, a, d]
        src = self.m.at[a, 0, d] if own else dst
        return (self.copy(src, dst, self.x_send.at[t], self.x_recv.at[t], self.nxt),
                self.copy(src, dst, self.p_send.at[t], self.p_recv.at[t], self.partner))

    def x_piece(self, t):
        @pl.when(jnp.logical_not(self.has_prev))
        def _():
            chain, side = self.x_copies(t, True)
            chain.start()
            side.start()

        @pl.when(self.has_prev)
        def _():
            chain, side = self.x_copies(t, False)
            chain.wait_recv()

            @pl.when(self.has_next)
            def _():
                chain.start()
            side.start()

    def x_other(self, t):
        a, d = self.part(t, PIECES)
        ref = self.cols.at[1 - self.core, a, d]
        self.copy(ref, ref, self.p_send.at[t], self.p_recv.at[t], self.partner).wait_recv()

    def r_copy(self, k, u, src, is_up):
        c, d = self.part(u, R_PIECES)
        dst = self.rows.at[k, c, d]
        ref = {"own": lambda: self.m.at[0, c, d],
               "column": lambda: self.cols.at[k, (c * self.n_col + self.col) // self.n_row, d],
               "relay": lambda: dst}[src]()
        sem = (self.r_up if is_up else self.r_down).at[k, u]
        return self.copy(ref, dst, sem, self.r_recv.at[k, u], self.up if is_up else self.down)

    def r_roles(self, k):
        z, late, home = self.z, self.late, self.home
        early = jnp.logical_not(late)
        top = self.n_row - 1
        own_up = (z == k) & jnp.where(late, z + 1 < PANELS, z < top)
        own_down = (z == k) & (z > 0)
        column = late & (z == home)
        column_up = column & (z < top)
        column_down = column & (z > PANELS)
        relay_up = (early & (z > k) & (z < top)) | (late & (z > home) & (z < top))
        relay_down = late & (z > PANELS) & (z < home)
        arrives = jnp.where(late & (z >= PANELS), z != home, z != k)
        return own_up, own_down, column_up, column_down, relay_up, relay_down, arrives

    def r_begin(self):
        for k in range(PANELS):
            own_up, own_down, *_ = self.r_roles(k)
            for u in range(self.n_r):
                if k == 0 or u < self.n_r // 2:
                    @pl.when(own_up)
                    def _():
                        self.r_copy(k, u, "own", True).start()

                @pl.when(own_down)
                def _():
                    self.r_copy(k, u, "own", False).start()

    def r_piece(self, k, u):
        own_up, _, column_up, column_down, relay_up, relay_down, arrives = self.r_roles(k)
        if not (k == 0 or u < self.n_r // 2):
            @pl.when(own_up)
            def _():
                self.r_copy(k, u, "own", True).start()

        @pl.when(arrives)
        def _():
            self.r_copy(k, u, "relay", True).wait_recv()
        for cond, src, is_up in ((column_up, "column", True), (column_down, "column", False),
                                 (relay_up, "relay", True), (relay_down, "relay", False)):
            @pl.when(cond)
            def _():
                self.r_copy(k, u, src, is_up).start()

    ORIGIN = (0, 1, 1)
    CARRIER = (0, 0, 1)

    def l_copy(self, b, q, own, way):
        _, d = self.part(q, PIECES)
        dst = self.lead.at[b, d]
        src = self.cols.at[self.CARRIER[b], 0, d] if own else dst
        sem, dev = {"up": (self.l_up, self.up), "down": (self.l_down, self.down),
                    "beside": (self.l_side, self.beside)}[way]
        return self.copy(src, dst, sem.at[b, q], self.l_recv.at[b, q], dev)

    def l_partner(self, b, q):
        _, d = self.part(q, PIECES)
        ref = self.lead.at[b, d]
        return self.copy(ref, ref, self.lp_send.at[b, q], self.lp_recv.at[b, q], self.partner)

    def l_start(self, b, q):
        @pl.when((self.z == self.ORIGIN[b]) & (self.core == self.CARRIER[b]) & self.odd)
        def _():
            if self.ORIGIN[b] > 0:
                self.l_copy(b, q, True, "down").start()

            @pl.when(self.has_up)
            def _():
                self.l_copy(b, q, True, "up").start()

    def l_relay(self, b, q):
        away = self.z != self.ORIGIN[b]
        mine = self.core == self.CARRIER[b]

        @pl.when(away & mine)
        def _():
            self.l_copy(b, q, False, "up").wait_recv()

            @pl.when(self.odd)
            def _():
                @pl.when((self.z > self.ORIGIN[b]) & self.has_up)
                def _():
                    self.l_copy(b, q, False, "up").start()
                self.l_copy(b, q, False, "beside").start()
            self.l_partner(b, q).start()

        @pl.when(away & jnp.logical_not(mine))
        def _():
            self.l_partner(b, q).wait_recv()

    def drain(self):
        for t in range(self.n_x):
            chain, side = self.x_copies(t, False)
            side.wait_send()

            @pl.when(self.has_next)
            def _():
                chain.wait_send()
        for k in range(PANELS):
            own_up, own_down, column_up, column_down, relay_up, relay_down, _ = self.r_roles(k)
            for u in range(self.n_r):
                @pl.when(own_up | column_up | relay_up)
                def _():
                    self.r_copy(k, u, "relay", True).wait_send()

                @pl.when(own_down | column_down | relay_down)
                def _():
                    self.r_copy(k, u, "relay", False).wait_send()
        for b in range(3):
            mine = self.core == self.CARRIER[b]
            away = self.z != self.ORIGIN[b]
            for q in range(PIECES):
                @pl.when(mine & self.odd & (self.z >= self.ORIGIN[b]) & self.has_up)
                def _():
                    self.l_copy(b, q, False, "up").wait_send()
                if self.ORIGIN[b] > 0:
                    @pl.when(mine & self.odd & (self.z == self.ORIGIN[b]))
                    def _():
                        self.l_copy(b, q, False, "down").wait_send()

                @pl.when(mine & self.odd & away)
                def _():
                    self.l_copy(b, q, False, "beside").wait_send()

                @pl.when(mine & away)
                def _():
                    self.l_partner(b, q).wait_send()


def factor_small(s_ref, hook):
    n = s_ref.shape[0]
    lane = lax.broadcasted_iota(jnp.int32, (GROUP, n), 1)

    def step(i, carry):
        base = pl.multiple_of(i * GROUP, GROUP)
        g = s_ref[pl.ds(base, GROUP), :]
        diag = pltpu.roll(g[:, :n], lax.rem(n - base, n), 1)
        t = {}
        for a in range(GROUP):
            for b in range(a + 1):
                t[a, b] = jnp.broadcast_to(diag[b:b + 1, a:a + 1], (1, n))
        left = [g[a:a + 1, :n] for a in range(GROUP)]
        right = [g[a:a + 1, n:] for a in range(GROUP)]
        for k in range(GROUP):
            r = lax.rsqrt(t[k, k])
            left[k] = left[k] * r
            right[k] = right[k] * r
            col = {a: t[a, k] * r for a in range(k + 1, GROUP)}
            for a in range(k + 1, GROUP):
                for b in range(k + 1, a + 1):
                    t[a, b] = t[a, b] - col[a] * col[b]
            for a in range(k + 1, GROUP):
                left[a] = left[a] - col[a] * left[k]
                right[a] = right[a] - col[a] * right[k]
        u = jnp.concatenate(left, axis=0)
        v = jnp.concatenate(right, axis=0)
        done = jnp.concatenate([u, v], axis=1)
        s_ref[pl.ds(base, GROUP), :] = done

        def split(w):
            h = w.astype(jnp.bfloat16).astype(jnp.float32)
            rest = w - h
            m = rest.astype(jnp.bfloat16).astype(jnp.float32)
            return h, m, rest - m

        h, m, l = split(done)
        keep = lane >= base + GROUP
        hm, mm_, lm = (jnp.where(keep, w[:, :n], 0.0) for w in (h, m, l))
        lhs = jnp.concatenate([hm, hm, mm_, hm, lm, mm_], axis=0).astype(jnp.bfloat16)
        rhs = jnp.concatenate([h, m, h, l, h, m], axis=0).astype(jnp.bfloat16)
        s_ref[...] -= lax.dot_general(
            lhs, rhs, (((0,), (0,)), ((), ())), preferred_element_type=jnp.float32
        )
        return carry

    for start in range(0, n // GROUP, STEPS):
        hook()
        lax.fori_loop(start, min(start + STEPS, n // GROUP), step, 0)


def factor(src, low, inv, s_ref, hook):
    size = src.shape[0]
    n = s_ref.shape[0]
    row = lax.broadcasted_iota(jnp.int32, (n, n), 0)
    lane = lax.broadcasted_iota(jnp.int32, (n, n), 1)
    eye = jnp.where(row == lane, 1.0, 0.0)
    low[...] = jnp.zeros_like(low)
    inv[...] = jnp.zeros_like(inv)
    for b in range(size // n):
        at = slice(b * n, (b + 1) * n)
        s_ref[:, :n] = src[at, at]
        s_ref[:, n:] = eye
        factor_small(s_ref, hook)
        v = jnp.where(row >= lane, s_ref[:, n:], 0.0)
        low[at, at] = jnp.where(row <= lane, s_ref[:, :n], 0.0).T
        inv[at, at] = v
        if b > 0:
            inv[at, :b * n] = -mm(v, mm(low[at, :b * n], inv[:b * n, :b * n]))
        if (b + 1) * n < size:
            below = mm_nt(src[(b + 1) * n:, at], v)
            low[(b + 1) * n:, at] = below
            src[(b + 1) * n:, (b + 1) * n:] -= mm_nt(below, below)


def hooks(ex):
    every = [[] for _ in range(16)]
    for q in range(PIECES):
        every[q] += [functools.partial(ex.l_relay, 1, q), functools.partial(ex.l_relay, 2, q)]
    for i, t in enumerate(range(2 * PIECES, ex.n_x)):
        every[min(i * 3 // 4, 7)].append(functools.partial(ex.x_piece, t))
    for i, t in enumerate(range(PIECES, ex.n_x)):
        every[min(i * 3 // 4, 8)].append(functools.partial(ex.x_other, t))
    half = ex.n_r // 2
    order = [(k, h * half + u) for h in range(2) for k in (1, 0) for u in range(half)]
    when = [0, 2, 4, 6, 9, 11, 13, 15]
    for i, (k, u) in enumerate(order):
        every[when[min(i, 7)]].append(functools.partial(ex.r_piece, k, u))
    return every


def compute(shape, m_ref, out, cols, rows, lead, work, low, inv, l10, q, s_ref, *sems):
    n_row, n_col = shape
    z = lax.axis_index("row")
    col = lax.axis_index("col")
    blocks, per = m_ref.shape[0], m_ref.shape[1]
    ex = Exchange(shape, m_ref, cols, rows, lead, sems)
    for t in range(PIECES):
        ex.x_piece(t)
        for b in range(3):
            ex.l_start(b, t)
    ex.r_begin()

    @pl.when(jnp.logical_not(ex.has_prev))
    def _():
        for a in range(blocks):
            cols[ex.core, a] = m_ref[a, 0]

    for t in range(PIECES):
        ex.x_other(t)
    for t in range(PIECES):
        ex.l_relay(0, t)
        ex.x_piece(PIECES + t)
    todo = hooks(ex)

    def hook():
        if todo:
            for job in todo.pop(0):
                job()

    def leading(b):
        @pl.when(z == ex.ORIGIN[b])
        def _():
            lead[b] = cols[ex.CARRIER[b], 0]
        return lead[b]

    work[...] = leading(0)
    factor(work, low.at[0], inv.at[0], s_ref, hook)
    l10[...] = mm_nt(leading(1), inv[0])
    work[...] = leading(2) - mm_nt(l10[...], l10[...])
    factor(work, low.at[1], inv.at[1], s_ref, hook)
    while todo:
        hook()

    for k in range(PANELS):
        turned = ex.late & (z >= PANELS)

        @pl.when(z == k)
        def _():
            q[k] = m_ref[0]

        @pl.when((z != k) & jnp.logical_not(turned))
        def _():
            q[k] = rows[k]
        for c in range(per):
            @pl.when(turned & (z == ex.home))
            def _():
                q[k, c] = cols[k, (c * n_col + col) // n_row].T

            @pl.when(turned & (z != ex.home))
            def _():
                q[k, c] = rows[k, c].T

    for c in range(per):
        q[0, c] = mm(inv[0], q[0, c])
        q[1, c] = mm(inv[1], q[1, c] - mm(l10[...], q[0, c]))

    def block_row(a, carry):
        p0 = mm_nt(cols[0, a], inv[0])
        p1 = mm_nt(cols[1, a] - mm_nt(p0, l10[...]), inv[1])
        for c in range(per):
            out[a, c] = m_ref[a, c] - mm(p0, q[0, c]) - mm(p1, q[1, c])

        @pl.when(col == 0)
        def _():
            out[a, 0] = p0

        @pl.when(col == 1)
        def _():
            out[a, 0] = p1
        return carry

    lax.fori_loop(0, blocks, block_row, 0)

    @pl.when(z < PANELS)
    def _():
        out[0] = jnp.zeros_like(out[0])

        @pl.when((z == 0) & (col == 0))
        def _():
            out[0, 0] = low[0]

        @pl.when((z == 1) & (col == 0))
        def _():
            out[0, 0] = l10[...]

        @pl.when((z == 1) & (col == 1))
        def _():
            out[0, 0] = low[1]
    ex.drain()


def shards(shape, matrix):
    m = matrix.transpose(0, 2, 1, 3)
    blocks, per, size, _ = m.shape
    f32 = jnp.float32
    dma = pltpu.SemaphoreType.DMA
    n_x, n_r = blocks * PIECES, per * R_PIECES
    tile = 128
    vmem = pl.BlockSpec(memory_space=pltpu.VMEM)
    out = pl.pallas_call(
        functools.partial(compute, shape),
        out_shape=jax.ShapeDtypeStruct(m.shape, f32),
        in_specs=[vmem],
        out_specs=vmem,
        scratch_shapes=[
            pltpu.VMEM((PANELS, blocks, size, size), f32),
            pltpu.VMEM((PANELS, per, size, size), f32),
            pltpu.VMEM((3, size, size), f32),
            pltpu.VMEM((size, size), f32),
            pltpu.VMEM((PANELS, size, size), f32),
            pltpu.VMEM((PANELS, size, size), f32),
            pltpu.VMEM((size, size), f32),
            pltpu.VMEM((PANELS, per, size, size), f32),
            pltpu.VMEM((tile, 2 * tile), f32),
        ] + [dma((n_x,))] * 4 + [dma((3, PIECES))] * 6 + [dma((PANELS, n_r))] * 3,
        compiler_params=pltpu.CompilerParams(collective_id=0, has_side_effects=True),
        name="factor",
    )(m)
    return out.transpose(0, 2, 1, 3)


def solution(mesh):
    spec = P(None, "row", None, "col")
    shape = (mesh.shape["row"], mesh.shape["col"])
    return jax.shard_map(
        functools.partial(shards, shape), mesh=mesh, in_specs=(spec,), out_specs=spec, check_vma=False
    )
```

```python
import functools
import math

import jax
import jax.numpy as jnp
from jax import lax
from jax.experimental import pallas as pl
from jax.experimental.pallas import tpu as pltpu
from jax.sharding import PartitionSpec as P

MESH = pl.DeviceIdType.MESH
PANELS = 2
PIECES = 4
R_PIECES = 2
STEPS = 4
GROUP = 8
HIGHEST = lax.Precision.HIGHEST


def mm(a, b):
    return jnp.dot(a, b, precision=HIGHEST, preferred_element_type=jnp.float32)


def mm_nt(a, b):
    return lax.dot_general(
        a, b, (((1,), (1,)), ((), ())), precision=HIGHEST, preferred_element_type=jnp.float32
    )


def mm_tn(a, b):
    return lax.dot_general(
        a, b, (((0,), (0,)), ((), ())), precision=HIGHEST, preferred_element_type=jnp.float32
    )


def snake(pos, width):
    major, minor = pos // width, pos % width
    return major, jnp.where(major % 2 == 0, minor, width - 1 - minor)


class Exchange:
    def __init__(self, shape, m_ref, cols, rows, lead, sems):
        (self.x_send, self.x_recv, self.p_send, self.p_recv, self.l_up, self.l_down, self.l_side,
         self.l_recv, self.lp_send, self.lp_recv, self.r_up, self.r_down, self.r_recv) = sems
        self.m, self.cols, self.rows, self.lead = m_ref, cols, rows, lead
        n_row, n_col = shape
        self.n_row, self.n_col = shape
        chips = n_col // 2
        width = math.isqrt(chips)
        if width * width != chips:
            width = chips
        height = chips // width
        z = lax.axis_index("row")
        col = lax.axis_index("col")
        chip, core = col // 2, col % 2
        y, x = chip // width, chip % width
        pos_a = y * width + jnp.where(y % 2 == 0, x, width - 1 - x)
        pos_b = x * height + jnp.where(x % 2 == 0, y, height - 1 - y)
        pos = jnp.where(core == 0, pos_a, pos_b)

        def chip_at(p):
            ya, xa = snake(p, width)
            xb, yb = snake(p, height)
            return jnp.where(core == 0, ya * width + xa, yb * width + xb)

        last = chips - 1
        self.z, self.col, self.core = z, col, core
        self.odd = chip % 2 == 1
        self.partner = (z, chip * 2 + 1 - core)
        self.beside = (z, (chip + 1 - 2 * (chip % 2)) * 2 + core)
        self.has_next, self.has_prev = pos < last, pos > 0
        self.nxt = (z, chip_at(jnp.minimum(pos + 1, last)) * 2 + core)
        prv = (z, chip_at(jnp.maximum(pos - 1, 0)) * 2 + core)
        self.up, self.down = (z + 1, col), (z - 1, col)
        self.has_up, has_down = z < n_row - 1, z > 0
        self.blocks, self.per, self.size = m_ref.shape[0], m_ref.shape[1], m_ref.shape[2]
        self.n_x = self.blocks * PIECES
        self.n_r = self.per * R_PIECES
        self.home = col % n_row
        self.late = self.home >= PANELS

        barrier = pltpu.get_barrier_semaphore()

        def greet(cond, dev):
            @pl.when(cond)
            def _():
                pl.semaphore_signal(barrier, inc=1, device_id=dev, device_id_type=MESH)

        for dev in (self.partner, self.beside):
            pl.semaphore_signal(barrier, inc=1, device_id=dev, device_id_type=MESH)
        near = ((self.has_next, self.nxt), (self.has_prev, prv), (self.has_up, self.up),
                (has_down, self.down))
        count = 2
        for cond, dev in near:
            greet(cond, dev)
            count = count + jnp.where(cond, 1, 0)
        pl.semaphore_wait(barrier, count)

    def copy(self, src, dst, s, r, dev):
        return pltpu.make_async_remote_copy(
            src_ref=src, dst_ref=dst, send_sem=s, recv_sem=r, device_id=dev, device_id_type=MESH
        )

    def part(self, t, pieces):
        step = self.size // pieces
        return t // pieces, pl.ds((t % pieces) * step, step)

    def x_copies(self, t, own):
        a, d = self.part(t, PIECES)
        dst = self.cols.at[self.core, a, d]
        src = self.m.at[a, 0, d] if own else dst
        return (self.copy(src, dst, self.x_send.at[t], self.x_recv.at[t], self.nxt),
                self.copy(src, dst, self.p_send.at[t], self.p_recv.at[t], self.partner))

    def x_begin(self, t):
        @pl.when(jnp.logical_not(self.has_prev))
        def _():
            chain, side = self.x_copies(t, True)
            chain.start()
            side.start()

    def x_piece(self, t):
        @pl.when(self.has_prev)
        def _():
            chain, side = self.x_copies(t, False)
            chain.wait_recv()

            @pl.when(self.has_next)
            def _():
                chain.start()
            side.start()

    def x_other(self, t):
        a, d = self.part(t, PIECES)
        ref = self.cols.at[1 - self.core, a, d]
        self.copy(ref, ref, self.p_send.at[t], self.p_recv.at[t], self.partner).wait_recv()

    def r_copy(self, k, u, src, is_up):
        c, d = self.part(u, R_PIECES)
        dst = self.rows.at[k, c, d]
        ref = {"own": lambda: self.m.at[0, c, d],
               "column": lambda: self.cols.at[k, (c * self.n_col + self.col) // self.n_row, d],
               "relay": lambda: dst}[src]()
        sem = (self.r_up if is_up else self.r_down).at[k, u]
        return self.copy(ref, dst, sem, self.r_recv.at[k, u], self.up if is_up else self.down)

    def r_roles(self, k):
        z, late, home = self.z, self.late, self.home
        early = jnp.logical_not(late)
        top = self.n_row - 1
        own_up = (z == k) & jnp.where(late, z + 1 < PANELS, z < top)
        own_down = (z == k) & (z > 0)
        column = late & (z == home)
        column_up = column & (z < top)
        column_down = column & (z > PANELS)
        relay_up = (early & (z > k) & (z < top)) | (late & (z > home) & (z < top))
        relay_down = late & (z > PANELS) & (z < home)
        arrives = jnp.where(late & (z >= PANELS), z != home, z != k)
        return own_up, own_down, column_up, column_down, relay_up, relay_down, arrives

    def r_begin(self, cond):
        for k in range(PANELS):
            own_up, own_down, *_ = self.r_roles(k)
            for u in range(self.n_r):
                @pl.when(own_up & cond)
                def _():
                    self.r_copy(k, u, "own", True).start()

                @pl.when(own_down & cond)
                def _():
                    self.r_copy(k, u, "own", False).start()

    def r_piece(self, k, u, cond):
        _, _, column_up, column_down, relay_up, relay_down, arrives = (
            role & cond for role in self.r_roles(k)
        )

        @pl.when(arrives)
        def _():
            self.r_copy(k, u, "relay", True).wait_recv()
        for cond, src, is_up in ((column_up, "column", True), (column_down, "column", False),
                                 (relay_up, "relay", True), (relay_down, "relay", False)):
            @pl.when(cond)
            def _():
                self.r_copy(k, u, src, is_up).start()

    ORIGIN = (0, 1, 1)
    CARRIER = (0, 0, 1)

    def l_copy(self, b, q, own, way):
        _, d = self.part(q, PIECES)
        dst = self.lead.at[b, d]
        src = self.cols.at[self.CARRIER[b], 0, d] if own else dst
        sem, dev = {"up": (self.l_up, self.up), "down": (self.l_down, self.down),
                    "beside": (self.l_side, self.beside)}[way]
        return self.copy(src, dst, sem.at[b, q], self.l_recv.at[b, q], dev)

    def l_partner(self, b, q):
        _, d = self.part(q, PIECES)
        ref = self.lead.at[b, d]
        return self.copy(ref, ref, self.lp_send.at[b, q], self.lp_recv.at[b, q], self.partner)

    def l_start(self, b, q):
        @pl.when((self.z == self.ORIGIN[b]) & (self.core == self.CARRIER[b]) & self.odd)
        def _():
            if self.ORIGIN[b] > 0:
                self.l_copy(b, q, True, "down").start()

            @pl.when(self.has_up)
            def _():
                self.l_copy(b, q, True, "up").start()

    def l_relay(self, b, q):
        away = self.z != self.ORIGIN[b]
        mine = self.core == self.CARRIER[b]

        @pl.when(away & mine)
        def _():
            self.l_copy(b, q, False, "up").wait_recv()

            @pl.when(self.odd)
            def _():
                @pl.when((self.z > self.ORIGIN[b]) & self.has_up)
                def _():
                    self.l_copy(b, q, False, "up").start()
                self.l_copy(b, q, False, "beside").start()
            self.l_partner(b, q).start()

        @pl.when(away & jnp.logical_not(mine))
        def _():
            self.l_partner(b, q).wait_recv()

    def drain(self):
        for t in range(self.n_x):
            chain, side = self.x_copies(t, False)
            side.wait_send()

            @pl.when(self.has_next)
            def _():
                chain.wait_send()
        for k in range(PANELS):
            own_up, own_down, column_up, column_down, relay_up, relay_down, _ = self.r_roles(k)
            for u in range(self.n_r):
                @pl.when(own_up | column_up | relay_up)
                def _():
                    self.r_copy(k, u, "relay", True).wait_send()

                @pl.when(own_down | column_down | relay_down)
                def _():
                    self.r_copy(k, u, "relay", False).wait_send()
        for b in range(3):
            mine = self.core == self.CARRIER[b]
            away = self.z != self.ORIGIN[b]
            for q in range(PIECES):
                @pl.when(mine & self.odd & (self.z >= self.ORIGIN[b]) & self.has_up)
                def _():
                    self.l_copy(b, q, False, "up").wait_send()
                if self.ORIGIN[b] > 0:
                    @pl.when(mine & self.odd & (self.z == self.ORIGIN[b]))
                    def _():
                        self.l_copy(b, q, False, "down").wait_send()

                @pl.when(mine & self.odd & away)
                def _():
                    self.l_copy(b, q, False, "beside").wait_send()

                @pl.when(mine & away)
                def _():
                    self.l_partner(b, q).wait_send()


def factor_small(s_ref, hook):
    n = s_ref.shape[0]
    lane = lax.broadcasted_iota(jnp.int32, (GROUP, n), 1)

    def step(i, carry):
        base = pl.multiple_of(i * GROUP, GROUP)
        g = s_ref[pl.ds(base, GROUP), :]
        diag = pltpu.roll(g[:, :n], lax.rem(n - base, n), 1)
        t = {}
        for a in range(GROUP):
            for b in range(a + 1):
                t[a, b] = jnp.broadcast_to(diag[b:b + 1, a:a + 1], (1, n))
        left = [g[a:a + 1, :n] for a in range(GROUP)]
        right = [g[a:a + 1, n:] for a in range(GROUP)]
        for k in range(GROUP):
            r = lax.rsqrt(t[k, k])
            left[k] = left[k] * r
            right[k] = right[k] * r
            col = {a: t[a, k] * r for a in range(k + 1, GROUP)}
            for a in range(k + 1, GROUP):
                for b in range(k + 1, a + 1):
                    t[a, b] = t[a, b] - col[a] * col[b]
            for a in range(k + 1, GROUP):
                left[a] = left[a] - col[a] * left[k]
                right[a] = right[a] - col[a] * right[k]
        u = jnp.concatenate(left, axis=0)
        v = jnp.concatenate(right, axis=0)
        done = jnp.concatenate([u, v], axis=1)
        s_ref[pl.ds(base, GROUP), :] = done

        def split(w):
            h = w.astype(jnp.bfloat16).astype(jnp.float32)
            rest = w - h
            m = rest.astype(jnp.bfloat16).astype(jnp.float32)
            return h, m, rest - m

        h, m, l = split(done)
        keep = lane >= base + GROUP
        hm, mm_, lm = (jnp.where(keep, w[:, :n], 0.0) for w in (h, m, l))
        lhs = jnp.concatenate([hm, hm, mm_, hm, lm, mm_], axis=0).astype(jnp.bfloat16)
        rhs = jnp.concatenate([h, m, h, l, h, m], axis=0).astype(jnp.bfloat16)
        s_ref[...] -= lax.dot_general(
            lhs, rhs, (((0,), (0,)), ((), ())), preferred_element_type=jnp.float32
        )
        return carry

    for start in range(0, n // GROUP, STEPS):
        hook()
        lax.fori_loop(start, min(start + STEPS, n // GROUP), step, 0)


def factor(src, low, inv, s_ref, hook):
    size = src.shape[0]
    n = s_ref.shape[0]
    row = lax.broadcasted_iota(jnp.int32, (n, n), 0)
    lane = lax.broadcasted_iota(jnp.int32, (n, n), 1)
    eye = jnp.where(row == lane, 1.0, 0.0)
    low[...] = jnp.zeros_like(low)
    inv[...] = jnp.zeros_like(inv)
    for b in range(size // n):
        at = slice(b * n, (b + 1) * n)
        s_ref[:, :n] = src[at, at]
        s_ref[:, n:] = eye
        factor_small(s_ref, hook)
        v = jnp.where(row >= lane, s_ref[:, n:], 0.0)
        low[at, at] = jnp.where(row <= lane, s_ref[:, :n], 0.0).T
        inv[at, at] = v
        if b > 0:
            inv[at, :b * n] = -mm(v, mm(low[at, :b * n], inv[:b * n, :b * n]))
        if (b + 1) * n < size:
            below = mm_nt(src[(b + 1) * n:, at], v)
            low[(b + 1) * n:, at] = below
            src[(b + 1) * n:, (b + 1) * n:] -= mm_nt(below, below)


def hooks(ex):
    every = [[] for _ in range(16)]
    for i, t in enumerate(range(PIECES, ex.n_x)):
        every[min(i // 2, 7)].append(functools.partial(ex.x_piece, t))
        every[min(i // 2 + 1, 8)].append(functools.partial(ex.x_other, t))
    half = ex.n_r // 2
    order = [(k, h * half + u) for h in range(2) for k in (1, 0) for u in range(half)]
    first = ex.z < PANELS
    classes = (
        (jnp.logical_not(ex.late) & first, (0,) * 8),
        (jnp.logical_not(ex.late) & jnp.logical_not(first), (1, 2, 6, 7, 2, 3, 9, 12)),
        (ex.late & first, (6,) * 8),
        (ex.late & jnp.logical_not(first), (3, 3, 4, 4, 8, 8, 9, 9)),
    )
    for cond, when in classes:
        for i, (k, u) in enumerate(order):
            every[when[min(i, 7)]].append(functools.partial(ex.r_piece, k, u, cond))
    return every


def compute(shape, m_ref, out, cols, rows, lead, work, low, inv, l10, q, s_ref, *sems):
    n_row, n_col = shape
    z = lax.axis_index("row")
    col = lax.axis_index("col")
    blocks, per = m_ref.shape[0], m_ref.shape[1]
    ex = Exchange(shape, m_ref, cols, rows, lead, sems)
    for t in range(ex.n_x):
        ex.x_begin(t)
    ex.r_begin(jnp.logical_not(ex.late))
    for t in range(PIECES):
        ex.x_piece(t)
        for b in range(3):
            ex.l_start(b, t)

    @pl.when(jnp.logical_not(ex.has_prev))
    def _():
        for a in range(blocks):
            cols[ex.core, a] = m_ref[a, 0]

    for b in range(3):
        for t in range(PIECES):
            ex.l_relay(b, t)
    ex.r_begin(ex.late)
    for t in range(PIECES):
        ex.x_other(t)
    todo = hooks(ex)

    def hook():
        if todo:
            for job in todo.pop(0):
                job()

    def leading(b):
        @pl.when(z == ex.ORIGIN[b])
        def _():
            lead[b] = cols[ex.CARRIER[b], 0]
        return lead[b]

    work[...] = leading(0)
    factor(work, low.at[0], inv.at[0], s_ref, hook)
    l10[...] = mm_nt(leading(1), inv[0])
    work[...] = leading(2) - mm_nt(l10[...], l10[...])
    factor(work, low.at[1], inv.at[1], s_ref, hook)
    while todo:
        hook()

    for k in range(PANELS):
        turned = ex.late & (z >= PANELS)

        @pl.when(z == k)
        def _():
            q[k] = m_ref[0]

        @pl.when((z != k) & jnp.logical_not(turned))
        def _():
            q[k] = rows[k]
        for c in range(per):
            @pl.when(turned & (z == ex.home))
            def _():
                q[k, c] = cols[k, (c * n_col + col) // n_row].T

            @pl.when(turned & (z != ex.home))
            def _():
                q[k, c] = rows[k, c].T

    for c in range(per):
        q[0, c] = mm(inv[0], q[0, c])
        q[1, c] = mm(inv[1], q[1, c] - mm(l10[...], q[0, c]))

    def block_row(a, carry):
        p0 = mm_nt(cols[0, a], inv[0])
        p1 = mm_nt(cols[1, a] - mm_nt(p0, l10[...]), inv[1])
        for c in range(per):
            out[a, c] = m_ref[a, c] - mm(p0, q[0, c]) - mm(p1, q[1, c])

        @pl.when(col == 0)
        def _():
            out[a, 0] = p0

        @pl.when(col == 1)
        def _():
            out[a, 0] = p1
        return carry

    lax.fori_loop(0, blocks, block_row, 0)

    @pl.when(z < PANELS)
    def _():
        out[0] = jnp.zeros_like(out[0])

        @pl.when((z == 0) & (col == 0))
        def _():
            out[0, 0] = low[0]

        @pl.when((z == 1) & (col == 0))
        def _():
            out[0, 0] = l10[...]

        @pl.when((z == 1) & (col == 1))
        def _():
            out[0, 0] = low[1]
    ex.drain()


def shards(shape, matrix):
    m = matrix.transpose(0, 2, 1, 3)
    blocks, per, size, _ = m.shape
    f32 = jnp.float32
    dma = pltpu.SemaphoreType.DMA
    n_x, n_r = blocks * PIECES, per * R_PIECES
    tile = 128
    vmem = pl.BlockSpec(memory_space=pltpu.VMEM)
    out = pl.pallas_call(
        functools.partial(compute, shape),
        out_shape=jax.ShapeDtypeStruct(m.shape, f32),
        in_specs=[vmem],
        out_specs=vmem,
        scratch_shapes=[
            pltpu.VMEM((PANELS, blocks, size, size), f32),
            pltpu.VMEM((PANELS, per, size, size), f32),
            pltpu.VMEM((3, size, size), f32),
            pltpu.VMEM((size, size), f32),
            pltpu.VMEM((PANELS, size, size), f32),
            pltpu.VMEM((PANELS, size, size), f32),
            pltpu.VMEM((size, size), f32),
            pltpu.VMEM((PANELS, per, size, size), f32),
            pltpu.VMEM((tile, 2 * tile), f32),
        ] + [dma((n_x,))] * 4 + [dma((3, PIECES))] * 6 + [dma((PANELS, n_r))] * 3,
        compiler_params=pltpu.CompilerParams(collective_id=0, has_side_effects=True),
        name="factor",
    )(m)
    return out.transpose(0, 2, 1, 3)


def solution(mesh):
    spec = P(None, "row", None, "col")
    shape = (mesh.shape["row"], mesh.shape["col"])
    return jax.shard_map(
        functools.partial(shards, shape), mesh=mesh, in_specs=(spec,), out_specs=spec, check_vma=False
    )
```

```python
import functools
import math

import jax
import jax.numpy as jnp
from jax import lax
from jax.experimental import pallas as pl
from jax.experimental.pallas import tpu as pltpu
from jax.sharding import PartitionSpec as P

MESH = pl.DeviceIdType.MESH
PANELS = 2
PIECES = 4
R_PIECES = 2
STEPS = 4
GROUP = 8
HIGHEST = lax.Precision.HIGHEST


def mm(a, b):
    return jnp.dot(a, b, precision=HIGHEST, preferred_element_type=jnp.float32)


def mm_nt(a, b):
    return lax.dot_general(
        a, b, (((1,), (1,)), ((), ())), precision=HIGHEST, preferred_element_type=jnp.float32
    )


def mm_tn(a, b):
    return lax.dot_general(
        a, b, (((0,), (0,)), ((), ())), precision=HIGHEST, preferred_element_type=jnp.float32
    )


def snake(pos, width):
    major, minor = pos // width, pos % width
    return major, jnp.where(major % 2 == 0, minor, width - 1 - minor)


class Exchange:
    def __init__(self, shape, m_ref, cols, rows, lead, sems):
        (self.x_send, self.x_recv, self.p_send, self.p_recv, self.l_up, self.l_down, self.l_side,
         self.l_recv, self.lp_send, self.lp_recv, self.r_up, self.r_down, self.r_recv) = sems
        self.m, self.cols, self.rows, self.lead = m_ref, cols, rows, lead
        n_row, n_col = shape
        self.n_row, self.n_col = shape
        chips = n_col // 2
        width = math.isqrt(chips)
        if width * width != chips:
            width = chips
        height = chips // width
        z = lax.axis_index("row")
        col = lax.axis_index("col")
        chip, core = col // 2, col % 2
        y, x = chip // width, chip % width
        pos_a = y * width + jnp.where(y % 2 == 0, x, width - 1 - x)
        pos_b = x * height + jnp.where(x % 2 == 0, y, height - 1 - y)
        pos = jnp.where(core == 0, pos_a, pos_b)

        def chip_at(p):
            ya, xa = snake(p, width)
            xb, yb = snake(p, height)
            return jnp.where(core == 0, ya * width + xa, yb * width + xb)

        last = chips - 1
        self.z, self.col, self.core = z, col, core
        self.odd = chip % 2 == 1
        self.partner = (z, chip * 2 + 1 - core)
        self.beside = (z, (chip + 1 - 2 * (chip % 2)) * 2 + core)
        self.has_next, self.has_prev = pos < last, pos > 0
        self.nxt = (z, chip_at(jnp.minimum(pos + 1, last)) * 2 + core)
        prv = (z, chip_at(jnp.maximum(pos - 1, 0)) * 2 + core)
        self.up, self.down = (z + 1, col), (z - 1, col)
        self.has_up, has_down = z < n_row - 1, z > 0
        self.blocks, self.per, self.size = m_ref.shape[0], m_ref.shape[1], m_ref.shape[2]
        self.n_x = self.blocks * PIECES
        self.n_r = self.per * R_PIECES
        self.home = col % n_row
        self.late = self.home >= PANELS

        barrier = pltpu.get_barrier_semaphore()

        def greet(cond, dev):
            @pl.when(cond)
            def _():
                pl.semaphore_signal(barrier, inc=1, device_id=dev, device_id_type=MESH)

        for dev in (self.partner, self.beside):
            pl.semaphore_signal(barrier, inc=1, device_id=dev, device_id_type=MESH)
        near = ((self.has_next, self.nxt), (self.has_prev, prv), (self.has_up, self.up),
                (has_down, self.down))
        count = 2
        for cond, dev in near:
            greet(cond, dev)
            count = count + jnp.where(cond, 1, 0)
        pl.semaphore_wait(barrier, count)

    def copy(self, src, dst, s, r, dev):
        return pltpu.make_async_remote_copy(
            src_ref=src, dst_ref=dst, send_sem=s, recv_sem=r, device_id=dev, device_id_type=MESH
        )

    def part(self, t, pieces):
        step = self.size // pieces
        return t // pieces, pl.ds((t % pieces) * step, step)

    def x_copies(self, t, own):
        a, d = self.part(t, PIECES)
        dst = self.cols.at[self.core, a, d]
        src = self.m.at[a, 0, d] if own else dst
        return (self.copy(src, dst, self.x_send.at[t], self.x_recv.at[t], self.nxt),
                self.copy(src, dst, self.p_send.at[t], self.p_recv.at[t], self.partner))

    def x_piece(self, t):
        @pl.when(jnp.logical_not(self.has_prev))
        def _():
            chain, side = self.x_copies(t, True)
            chain.start()
            side.start()

        @pl.when(self.has_prev)
        def _():
            chain, side = self.x_copies(t, False)
            chain.wait_recv()

            @pl.when(self.has_next)
            def _():
                chain.start()
            side.start()

    def x_other(self, t):
        a, d = self.part(t, PIECES)
        ref = self.cols.at[1 - self.core, a, d]
        self.copy(ref, ref, self.p_send.at[t], self.p_recv.at[t], self.partner).wait_recv()

    def r_copy(self, k, u, src, is_up):
        c, d = self.part(u, R_PIECES)
        dst = self.rows.at[k, c, d]
        ref = {"own": lambda: self.m.at[0, c, d],
               "column": lambda: self.cols.at[k, (c * self.n_col + self.col) // self.n_row, d],
               "relay": lambda: dst}[src]()
        sem = (self.r_up if is_up else self.r_down).at[k, u]
        return self.copy(ref, dst, sem, self.r_recv.at[k, u], self.up if is_up else self.down)

    def r_roles(self, k):
        z, late, home = self.z, self.late, self.home
        early = jnp.logical_not(late)
        top = self.n_row - 1
        own_up = (z == k) & jnp.where(late, z + 1 < PANELS, z < top)
        own_down = (z == k) & (z > 0)
        column = late & (z == home)
        column_up = column & (z < top)
        column_down = column & (z > PANELS)
        relay_up = (early & (z > k) & (z < top)) | (late & (z > home) & (z < top))
        relay_down = late & (z > PANELS) & (z < home)
        arrives = jnp.where(late & (z >= PANELS), z != home, z != k)
        return own_up, own_down, column_up, column_down, relay_up, relay_down, arrives

    def r_begin(self):
        for k in range(PANELS):
            own_up, own_down, *_ = self.r_roles(k)
            for u in range(self.n_r):
                if k == 0 or u < self.n_r // 2:
                    @pl.when(own_up)
                    def _():
                        self.r_copy(k, u, "own", True).start()

                @pl.when(own_down)
                def _():
                    self.r_copy(k, u, "own", False).start()

    def r_piece(self, k, u):
        own_up, _, column_up, column_down, relay_up, relay_down, arrives = self.r_roles(k)
        if not (k == 0 or u < self.n_r // 2):
            @pl.when(own_up)
            def _():
                self.r_copy(k, u, "own", True).start()

        @pl.when(arrives)
        def _():
            self.r_copy(k, u, "relay", True).wait_recv()
        for cond, src, is_up in ((column_up, "column", True), (column_down, "column", False),
                                 (relay_up, "relay", True), (relay_down, "relay", False)):
            @pl.when(cond)
            def _():
                self.r_copy(k, u, src, is_up).start()

    ORIGIN = (0, 1, 1)
    CARRIER = (0, 0, 1)

    def l_copy(self, b, q, own, way):
        _, d = self.part(q, PIECES)
        dst = self.lead.at[b, d]
        src = self.cols.at[self.CARRIER[b], 0, d] if own else dst
        sem, dev = {"up": (self.l_up, self.up), "down": (self.l_down, self.down),
                    "beside": (self.l_side, self.beside)}[way]
        return self.copy(src, dst, sem.at[b, q], self.l_recv.at[b, q], dev)

    def l_partner(self, b, q):
        _, d = self.part(q, PIECES)
        ref = self.lead.at[b, d]
        return self.copy(ref, ref, self.lp_send.at[b, q], self.lp_recv.at[b, q], self.partner)

    def l_start(self, b, q):
        @pl.when((self.z == self.ORIGIN[b]) & (self.core == self.CARRIER[b]) & self.odd)
        def _():
            if self.ORIGIN[b] > 0:
                self.l_copy(b, q, True, "down").start()

            @pl.when(self.has_up)
            def _():
                self.l_copy(b, q, True, "up").start()

    def l_relay(self, b, q):
        away = self.z != self.ORIGIN[b]
        mine = self.core == self.CARRIER[b]

        @pl.when(away & mine)
        def _():
            self.l_copy(b, q, False, "up").wait_recv()

            @pl.when(self.odd)
            def _():
                @pl.when((self.z > self.ORIGIN[b]) & self.has_up)
                def _():
                    self.l_copy(b, q, False, "up").start()
                self.l_copy(b, q, False, "beside").start()
            self.l_partner(b, q).start()

        @pl.when(away & jnp.logical_not(mine))
        def _():
            self.l_partner(b, q).wait_recv()

    def drain(self):
        for t in range(self.n_x):
            chain, side = self.x_copies(t, False)
            side.wait_send()

            @pl.when(self.has_next)
            def _():
                chain.wait_send()
        for k in range(PANELS):
            own_up, own_down, column_up, column_down, relay_up, relay_down, _ = self.r_roles(k)
            for u in range(self.n_r):
                @pl.when(own_up | column_up | relay_up)
                def _():
                    self.r_copy(k, u, "relay", True).wait_send()

                @pl.when(own_down | column_down | relay_down)
                def _():
                    self.r_copy(k, u, "relay", False).wait_send()
        for b in range(3):
            mine = self.core == self.CARRIER[b]
            away = self.z != self.ORIGIN[b]
            for q in range(PIECES):
                @pl.when(mine & self.odd & (self.z >= self.ORIGIN[b]) & self.has_up)
                def _():
                    self.l_copy(b, q, False, "up").wait_send()
                if self.ORIGIN[b] > 0:
                    @pl.when(mine & self.odd & (self.z == self.ORIGIN[b]))
                    def _():
                        self.l_copy(b, q, False, "down").wait_send()

                @pl.when(mine & self.odd & away)
                def _():
                    self.l_copy(b, q, False, "beside").wait_send()

                @pl.when(mine & away)
                def _():
                    self.l_partner(b, q).wait_send()


def factor_small(s_ref, hook):
    n = s_ref.shape[0]
    lane = lax.broadcasted_iota(jnp.int32, (GROUP, n), 1)

    def step(i, carry):
        base = pl.multiple_of(i * GROUP, GROUP)
        g = s_ref[pl.ds(base, GROUP), :]
        diag = pltpu.roll(g[:, :n], lax.rem(n - base, n), 1)
        t = {}
        for a in range(GROUP):
            for b in range(a + 1):
                t[a, b] = jnp.broadcast_to(diag[b:b + 1, a:a + 1], (1, n))
        left = [g[a:a + 1, :n] for a in range(GROUP)]
        right = [g[a:a + 1, n:] for a in range(GROUP)]
        for k in range(GROUP):
            r = lax.rsqrt(t[k, k])
            left[k] = left[k] * r
            right[k] = right[k] * r
            col = {a: t[a, k] * r for a in range(k + 1, GROUP)}
            for a in range(k + 1, GROUP):
                for b in range(k + 1, a + 1):
                    t[a, b] = t[a, b] - col[a] * col[b]
            for a in range(k + 1, GROUP):
                left[a] = left[a] - col[a] * left[k]
                right[a] = right[a] - col[a] * right[k]
        u = jnp.concatenate(left, axis=0)
        v = jnp.concatenate(right, axis=0)
        done = jnp.concatenate([u, v], axis=1)
        s_ref[pl.ds(base, GROUP), :] = done

        def split(w):
            h = w.astype(jnp.bfloat16).astype(jnp.float32)
            rest = w - h
            m = rest.astype(jnp.bfloat16).astype(jnp.float32)
            return h, m, rest - m

        h, m, l = split(done)
        keep = lane >= base + GROUP
        hm, mm_, lm = (jnp.where(keep, w[:, :n], 0.0) for w in (h, m, l))
        lhs = jnp.concatenate([hm, hm, mm_, hm, lm, mm_], axis=0).astype(jnp.bfloat16)
        rhs = jnp.concatenate([h, m, h, l, h, m], axis=0).astype(jnp.bfloat16)
        s_ref[...] -= lax.dot_general(
            lhs, rhs, (((0,), (0,)), ((), ())), preferred_element_type=jnp.float32
        )
        return carry

    for start in range(0, n // GROUP, STEPS):
        hook()
        lax.fori_loop(start, min(start + STEPS, n // GROUP), step, 0)


def factor(src, low, inv, s_ref, hook):
    size = src.shape[0]
    n = s_ref.shape[0]
    row = lax.broadcasted_iota(jnp.int32, (n, n), 0)
    lane = lax.broadcasted_iota(jnp.int32, (n, n), 1)
    eye = jnp.where(row == lane, 1.0, 0.0)
    low[...] = jnp.zeros_like(low)
    inv[...] = jnp.zeros_like(inv)
    for b in range(size // n):
        at = slice(b * n, (b + 1) * n)
        s_ref[:, :n] = src[at, at]
        s_ref[:, n:] = eye
        factor_small(s_ref, hook)
        v = jnp.where(row >= lane, s_ref[:, n:], 0.0)
        low[at, at] = jnp.where(row <= lane, s_ref[:, :n], 0.0).T
        inv[at, at] = v
        if b > 0:
            inv[at, :b * n] = -mm(v, mm(low[at, :b * n], inv[:b * n, :b * n]))
        if (b + 1) * n < size:
            below = mm_nt(src[(b + 1) * n:, at], v)
            low[(b + 1) * n:, at] = below
            src[(b + 1) * n:, (b + 1) * n:] -= mm_nt(below, below)


def hooks(ex):
    every = [[] for _ in range(16)]
    for i, t in enumerate(range(2 * PIECES, ex.n_x)):
        every[min(i * 3 // 4, 7)].append(functools.partial(ex.x_piece, t))
    for i, t in enumerate(range(PIECES, ex.n_x)):
        every[min(i * 3 // 4, 8)].append(functools.partial(ex.x_other, t))
    half = ex.n_r // 2
    order = [(k, h * half + u) for h in range(2) for k in (1, 0) for u in range(half)]
    when = [0, 2, 4, 6, 9, 11, 13, 15]
    for i, (k, u) in enumerate(order):
        every[when[min(i, 7)]].append(functools.partial(ex.r_piece, k, u))
    return every


def compute(shape, m_ref, out, cols, rows, lead, work, low, inv, l10, q, s_ref, *sems):
    n_row, n_col = shape
    z = lax.axis_index("row")
    col = lax.axis_index("col")
    blocks, per = m_ref.shape[0], m_ref.shape[1]
    ex = Exchange(shape, m_ref, cols, rows, lead, sems)
    for t in range(PIECES):
        ex.x_piece(t)
        for b in range(3):
            ex.l_start(b, t)
    @pl.when(jnp.logical_not(ex.has_prev))
    def _():
        for a in range(blocks):
            cols[ex.core, a] = m_ref[a, 0]

    for t in range(PIECES):
        ex.x_other(t)
    for t in range(PIECES):
        ex.l_relay(0, t)
    for t in range(PIECES):
        ex.l_relay(1, t)
        ex.l_relay(2, t)
    for t in range(PIECES):
        ex.x_piece(PIECES + t)
    ex.r_begin()
    todo = hooks(ex)

    def hook():
        if todo:
            for job in todo.pop(0):
                job()

    def leading(b):
        @pl.when(z == ex.ORIGIN[b])
        def _():
            lead[b] = cols[ex.CARRIER[b], 0]
        return lead[b]

    work[...] = leading(0)
    factor(work, low.at[0], inv.at[0], s_ref, hook)
    l10[...] = mm_nt(leading(1), inv[0])
    work[...] = leading(2) - mm_nt(l10[...], l10[...])
    factor(work, low.at[1], inv.at[1], s_ref, hook)
    while todo:
        hook()

    for k in range(PANELS):
        turned = ex.late & (z >= PANELS)

        @pl.when(z == k)
        def _():
            q[k] = m_ref[0]

        @pl.when((z != k) & jnp.logical_not(turned))
        def _():
            q[k] = rows[k]
        for c in range(per):
            @pl.when(turned & (z == ex.home))
            def _():
                q[k, c] = cols[k, (c * n_col + col) // n_row].T

            @pl.when(turned & (z != ex.home))
            def _():
                q[k, c] = rows[k, c].T

    for c in range(per):
        q[0, c] = mm(inv[0], q[0, c])
        q[1, c] = mm(inv[1], q[1, c] - mm(l10[...], q[0, c]))

    def block_row(a, carry):
        p0 = mm_nt(cols[0, a], inv[0])
        p1 = mm_nt(cols[1, a] - mm_nt(p0, l10[...]), inv[1])
        for c in range(per):
            out[a, c] = m_ref[a, c] - mm(p0, q[0, c]) - mm(p1, q[1, c])

        @pl.when(col == 0)
        def _():
            out[a, 0] = p0

        @pl.when(col == 1)
        def _():
            out[a, 0] = p1
        return carry

    lax.fori_loop(0, blocks, block_row, 0)

    @pl.when(z < PANELS)
    def _():
        out[0] = jnp.zeros_like(out[0])

        @pl.when((z == 0) & (col == 0))
        def _():
            out[0, 0] = low[0]

        @pl.when((z == 1) & (col == 0))
        def _():
            out[0, 0] = l10[...]

        @pl.when((z == 1) & (col == 1))
        def _():
            out[0, 0] = low[1]
    ex.drain()


def shards(shape, matrix):
    m = matrix.transpose(0, 2, 1, 3)
    blocks, per, size, _ = m.shape
    f32 = jnp.float32
    dma = pltpu.SemaphoreType.DMA
    n_x, n_r = blocks * PIECES, per * R_PIECES
    tile = 128
    vmem = pl.BlockSpec(memory_space=pltpu.VMEM)
    out = pl.pallas_call(
        functools.partial(compute, shape),
        out_shape=jax.ShapeDtypeStruct(m.shape, f32),
        in_specs=[vmem],
        out_specs=vmem,
        scratch_shapes=[
            pltpu.VMEM((PANELS, blocks, size, size), f32),
            pltpu.VMEM((PANELS, per, size, size), f32),
            pltpu.VMEM((3, size, size), f32),
            pltpu.VMEM((size, size), f32),
            pltpu.VMEM((PANELS, size, size), f32),
            pltpu.VMEM((PANELS, size, size), f32),
            pltpu.VMEM((size, size), f32),
            pltpu.VMEM((PANELS, per, size, size), f32),
            pltpu.VMEM((tile, 2 * tile), f32),
        ] + [dma((n_x,))] * 4 + [dma((3, PIECES))] * 6 + [dma((PANELS, n_r))] * 3,
        compiler_params=pltpu.CompilerParams(collective_id=0, has_side_effects=True),
        name="factor",
    )(m)
    return out.transpose(0, 2, 1, 3)


def solution(mesh):
    spec = P(None, "row", None, "col")
    shape = (mesh.shape["row"], mesh.shape["col"])
    return jax.shard_map(
        functools.partial(shards, shape), mesh=mesh, in_specs=(spec,), out_specs=spec, check_vma=False
    )
```
